32 devices in a mesh: grp: 2 (over x), lat: 2 (over core), lon: 8 (over z, y).
Axes of the slice: x: 2, y: 2, z: 4, core: 2. Of those that a mesh axis runs over, the one named last changes fastest.
Arguments:
- fields: bfloat16 [256, 128, 768], P(('grp', 'lat'), 'lon'), parts along dimension 0, may hold values from -6 to 6
- ocean: int32 [256, 128], P(('grp', 'lat'), 'lon'), parts along dimension 0, may hold values 0 or 1
- w_query1: bfloat16 [768, 768], replicated, may hold values from -4 to 4
- w_key1: bfloat16 [768, 768], replicated, may hold values from -4 to 4
- w_value1: bfloat16 [768, 768], replicated, may hold values from -0.21875 to 0.21875
- w_out1: bfloat16 [768, 768], replicated, may hold values from -0.21875 to 0.21875
- w_query2: bfloat16 [768, 768], replicated, may hold values from -4 to 4
- w_key2: bfloat16 [768, 768], replicated, may hold values from -4 to 4
- w_value2: bfloat16 [768, 768], replicated, may hold values from -0.21875 to 0.21875
- w_out2: bfloat16 [768, 768], replicated, may hold values from -0.21875 to 0.21875
Outputs:
- forecast: bfloat16 [256, 128, 768], P(('grp', 'lat'), 'lon'), parts along dimension 0
The draws below stay inside these ranges and needn't reach their ends.
There are 2 independent parts, one for each index of `grp`. The reference program is written for one: setup_inputs(seed, part) draws one part's arguments, and reference() takes and returns one part's arrays. A program takes and returns all parts, laid end to end along the dimension named above; an argument that names none is the same for every part. Nothing has to cross between parts.
All inputs are finite; a program needn't handle non-finite values. No bound on the sum of `ocean` on one device may be relied on, other than what follows from the above.
Results may differ from the reference program's by a relative error of at most 0.006.
Values may be sent and summed in bfloat16 or wider, within the bound.
A program may use at most 128 MiB of HBM per device.

```python
import jax
import jax.numpy as jnp
from jax import lax

D = 768
HEADS = 12
LATS = 128
LONS = 128


def weight_pair(key, salt):
    first = jax.random.normal(jax.random.fold_in(key, salt), (D, D), jnp.float32) * D ** (-0.5)
    second = jax.random.normal(jax.random.fold_in(key, salt + 1), (D, D), jnp.float32) * D ** (-0.5)
    return (jnp.clip(first, -4.0, 4.0), jnp.clip(second, -4.0, 4.0))


def draw_w_query1(key, part):
    return weight_pair(key, 101)[0].astype(jnp.bfloat16)


def draw_w_key1(key, part):
    return weight_pair(key, 101)[1].astype(jnp.bfloat16)


def draw_w_query2(key, part):
    return weight_pair(key, 203)[0].astype(jnp.bfloat16)


def draw_w_key2(key, part):
    return weight_pair(key, 203)[1].astype(jnp.bfloat16)


def touch_ends(drawn, own_key, smallest, largest):
    spot = [jax.random.randint(jax.random.fold_in(own_key, axis), (), 0, length) for axis, length in enumerate(drawn.shape)]
    main_axis = drawn.shape.index(max(drawn.shape))
    beside = spot[:main_axis] + [(spot[main_axis] + 1) % drawn.shape[main_axis]] + spot[main_axis + 1:]
    return drawn.at[tuple(spot)].set(smallest).at[tuple(beside)].set(largest)


def levels(own_key, dims, shards, least, largest):
    loudness = 1.0
    for position, parts in shards:
        heights = jax.random.uniform(jax.random.fold_in(jax.random.fold_in(own_key, 6), position), (parts,), jnp.float32, least / len(shards), largest / len(shards))
        loudness = loudness * jnp.repeat(jnp.exp(heights), dims[position] // parts).reshape((-1,) + (1,) * (len(dims) - 1 - position))
    return loudness


def centred(rng, shape, scale, limit, split=(), kind=jnp.bfloat16):
    drawn = scale * jax.random.normal(rng, shape, jnp.float32)
    if split:
        drawn = drawn * levels(rng, shape, split, -0.22, 0.18)
    return jnp.clip(drawn, -limit, limit).astype(kind)


def setup_inputs(seed: int = 0, part: int = 0) -> dict:
    key_of = jax.random.split(jax.random.key(seed), 11)
    own_keys = jax.random.split(jax.random.fold_in(key_of[10], part), 11)
    fields = centred(own_keys[0], (LATS, LONS, D), 1.0, 6.0, ((0, 2), (1, 8)))
    ocean = touch_ends((jax.random.randint(own_keys[1], (LATS, LONS), 0, 4) < 3).astype(jnp.int32), jax.random.fold_in(own_keys[1], 1), 0, 1)
    w_query1 = draw_w_query1(jax.random.fold_in(key_of[10], 71), part)
    w_key1 = draw_w_key1(jax.random.fold_in(key_of[10], 71), part)
    w_value1 = centred(key_of[4], (D, D), D ** -0.5, 0.21875)
    w_out1 = centred(key_of[5], (D, D), D ** -0.5, 0.21875)
    w_query2 = draw_w_query2(jax.random.fold_in(key_of[10], 71), part)
    w_key2 = draw_w_key2(jax.random.fold_in(key_of[10], 71), part)
    w_value2 = centred(key_of[8], (D, D), D ** -0.5, 0.21875)
    w_out2 = centred(key_of[9], (D, D), D ** -0.5, 0.21875)
    return dict(fields=fields, ocean=ocean, w_query1=w_query1, w_key1=w_key1, w_value1=w_value1, w_out1=w_out1, w_query2=w_query2, w_key2=w_key2, w_value2=w_value2, w_out2=w_out2)


EPS = 1e-05
NEG = -1e+30

def norm_rows(a):
    af = a.astype(jnp.float32)
    mean = lax.optimization_barrier(jnp.mean(af, -1, keepdims=True))
    var = lax.optimization_barrier(jnp.mean((af - mean) * (af - mean), -1, keepdims=True))
    return ((af - mean) * lax.rsqrt(var + EPS)).astype(jnp.bfloat16)

def project(h, weight):
    return jnp.dot(h, weight, preferred_element_type=jnp.float32).astype(jnp.bfloat16)

def masked_softmax(scores, key_ok, land_query):
    top = lax.optimization_barrier(jnp.max(jnp.where(key_ok, scores, NEG), -1, keepdims=True))
    expo = jnp.where(key_ok, jnp.exp(scores - top), 0.0)
    total = lax.optimization_barrier(jnp.sum(expo, -1, keepdims=True)) + land_query[..., None]
    return (expo / total).astype(jnp.bfloat16)

def window_attend(query, keys, values, flags):
    rows, cols, width = query.shape
    nh = HEADS
    hd = width // nh
    scale = hd ** (-0.5)

    def tiles(a):
        a = a.reshape(rows // 8, 8, cols // 8, 8, nh, hd).transpose(0, 2, 4, 1, 3, 5)
        return a.reshape(rows // 8, cols // 8, nh, 64, hd).astype(jnp.float32)
    marks = flags.reshape(rows // 8, 8, cols // 8, 8).transpose(0, 2, 1, 3).reshape(rows // 8, cols // 8, 64)
    key_ok = (marks > 0)[:, :, None, None, :]
    land_query = (marks <= 0).astype(jnp.float32)[:, :, None, :]
    scores = jnp.einsum('abhqd,abhkd->abhqk', tiles(query), tiles(keys)) * scale
    probs = masked_softmax(scores, key_ok, land_query)
    outs = jnp.einsum('abhqk,abhkd->abhqd', probs.astype(jnp.float32), tiles(values))
    outs = outs * (1.0 - land_query)[..., None]
    outs = outs.astype(jnp.bfloat16).reshape(rows // 8, cols // 8, nh, 8, 8, hd)
    return outs.transpose(0, 3, 1, 4, 2, 5).reshape(rows, cols, width)

def row_attend(query, keys, values, flags):
    rows, length, width = query.shape
    nh = HEADS
    hd = width // nh
    scale = hd ** (-0.5)
    key_ok = (flags > 0)[:, None, :]
    land_query = (flags <= 0).astype(jnp.float32)

    def head(index):
        qh = lax.dynamic_slice_in_dim(query, index * hd, hd, 2).astype(jnp.float32)
        kh = lax.dynamic_slice_in_dim(keys, index * hd, hd, 2).astype(jnp.float32)
        vh = lax.dynamic_slice_in_dim(values, index * hd, hd, 2).astype(jnp.float32)
        scores = jnp.einsum('rqd,rkd->rqk', qh, kh) * scale
        probs = masked_softmax(scores, key_ok, land_query)
        return jnp.einsum('rqk,rkd->rqd', probs.astype(jnp.float32), vh)
    outs = lax.map(head, jnp.arange(nh, dtype=jnp.int32))
    outs = outs.transpose(1, 2, 0, 3).reshape(rows, length, width)
    return (outs * (1.0 - land_query)[..., None]).astype(jnp.bfloat16)

def reference(fields, ocean, w_query1, w_key1, w_value1, w_out1, w_query2, w_key2, w_value2, w_out2):
    h1 = jnp.roll(norm_rows(fields), -4, 1)
    marks = jnp.roll(ocean, -4, 1)
    q1 = project(h1, w_query1)
    k1 = project(h1, w_key1)
    v1 = project(h1, w_value1)
    lats, lons, width = q1.shape

    def band(items):
        return window_attend(items[0], items[1], items[2], items[3])
    grouped = (q1.reshape(lats // 8, 8, lons, width), k1.reshape(lats // 8, 8, lons, width), v1.reshape(lats // 8, 8, lons, width), marks.reshape(lats // 8, 8, lons))
    o1 = jnp.roll(lax.map(band, grouped).reshape(lats, lons, width), 4, 1)
    y1 = (fields.astype(jnp.float32) + jnp.dot(o1, w_out1, preferred_element_type=jnp.float32)).astype(jnp.bfloat16)
    h2 = norm_rows(y1)
    q2 = project(h2, w_query2)
    k2 = project(h2, w_key2)
    v2 = project(h2, w_value2)

    def one_row(items):
        return row_attend(items[0][None], items[1][None], items[2][None], items[3][None])[0]
    o2 = lax.map(one_row, (q2, k2, v2, ocean))
    return (y1.astype(jnp.float32) + jnp.dot(o2, w_out2, preferred_element_type=jnp.float32)).astype(jnp.bfloat16)
```

```python
import jax
import jax.numpy as jnp
from jax import lax
from jax.experimental import pallas as pl
from jax.experimental.pallas import tpu as pltpu
from jax.sharding import PartitionSpec as P

HEADS = 12


EPS = 1e-05
NEG = -1e30


def passed_along(value, axis, steps):
    count = lax.axis_size(axis)
    pairs = [(source, (source + steps) % count) for source in range(count)]
    return lax.ppermute(value, axis, pairs)


def norm_rows(a):
    af = a.astype(jnp.float32)
    mean = jnp.mean(af, -1, keepdims=True)
    var = jnp.mean((af - mean) * (af - mean), -1, keepdims=True)
    return ((af - mean) * lax.rsqrt(var + EPS)).astype(jnp.bfloat16)


def project(h, weight):
    return jnp.dot(h, weight, preferred_element_type=jnp.float32).astype(jnp.bfloat16)


def masked_softmax(scores, key_ok, land_query):
    top = jnp.max(jnp.where(key_ok, scores, NEG), -1, keepdims=True)
    expo = jnp.where(key_ok, jnp.exp(scores - top), 0.0)
    total = jnp.sum(expo, -1, keepdims=True) + land_query[..., None]
    return (expo / total).astype(jnp.bfloat16)


def window_attend(query, keys, values, flags):
    rows, cols, width = query.shape
    nh = HEADS
    hd = width // nh
    scale = hd ** (-0.5)

    def tiles(a):
        a = a.reshape(rows // 8, 8, cols // 8, 8, nh, hd).transpose(0, 2, 4, 1, 3, 5)
        return a.reshape(rows // 8, cols // 8, nh, 64, hd)

    marks = (
        flags.reshape(rows // 8, 8, cols // 8, 8)
        .transpose(0, 2, 1, 3)
        .reshape(rows // 8, cols // 8, 64)
    )
    key_ok = (marks > 0)[:, :, None, None, :]
    land_query = (marks <= 0).astype(jnp.float32)[:, :, None, :]
    scores = (
        jnp.einsum(
            "abhqd,abhkd->abhqk", tiles(query), tiles(keys), preferred_element_type=jnp.float32
        )
        * scale
    )
    probs = masked_softmax(scores, key_ok, land_query)
    outs = jnp.einsum(
        "abhqk,abhkd->abhqd", probs, tiles(values), preferred_element_type=jnp.float32
    )
    outs = outs * (1.0 - land_query)[..., None]
    outs = outs.astype(jnp.bfloat16).reshape(rows // 8, cols // 8, nh, 8, 8, hd)
    return outs.transpose(0, 3, 1, 4, 2, 5).reshape(rows, cols, width)


def row_attend(query, keys, values, flags):
    rows, length, width = query.shape
    nh = HEADS
    hd = width // nh
    scale = hd ** (-0.5)
    key_ok = (flags > 0)[:, None, :]
    land_query = (flags <= 0).astype(jnp.float32)

    def head(index):
        qh = lax.dynamic_slice_in_dim(query, index * hd, hd, 2)
        kh = lax.dynamic_slice_in_dim(keys, index * hd, hd, 2)
        vh = lax.dynamic_slice_in_dim(values, index * hd, hd, 2)
        scores = jnp.einsum("rqd,rkd->rqk", qh, kh, preferred_element_type=jnp.float32) * scale
        probs = masked_softmax(scores, key_ok, land_query)
        return jnp.einsum("rqk,rkd->rqd", probs, vh, preferred_element_type=jnp.float32)

    outs = lax.map(head, jnp.arange(nh, dtype=jnp.int32))
    outs = outs.transpose(1, 2, 0, 3).reshape(rows, length, width)
    return (outs * (1.0 - land_query)[..., None]).astype(jnp.bfloat16)


def attend_columns(columns, marks, w_query1, w_key1, w_value1):
    return window_attend(
        project(columns, w_query1), project(columns, w_key1), project(columns, w_value1), marks
    )


def on_device(
    fields, ocean, w_query1, w_key1, w_value1, w_out1, w_query2, w_key2, w_value2, w_out2
):
    rows, cols, width = fields.shape
    normed = norm_rows(fields)
    marks = ocean.astype(jnp.bfloat16)
    edge_feats, edge_marks = passed_along((normed[:, cols - 4 :], marks[:, cols - 4 :]), "lon", 1)
    columns = jnp.concatenate([edge_feats, normed[:, : cols - 4]], 1)
    column_marks = jnp.concatenate([edge_marks, marks[:, : cols - 4]], 1)
    extended = attend_columns(columns, column_marks, w_query1, w_key1, w_value1)
    returned = passed_along(extended[:, :4], "lon", -1)
    o1 = jnp.concatenate([extended[:, 4:], returned], 1)
    y1 = (
        fields.astype(jnp.float32) + jnp.dot(o1, w_out1, preferred_element_type=jnp.float32)
    ).astype(jnp.bfloat16)
    h2 = norm_rows(y1)
    q2 = project(h2, w_query2)
    k2 = project(h2, w_key2)
    v2 = project(h2, w_value2)
    row_q, row_k, row_v, row_marks = (
        lax.all_to_all(q2, "lon", split_axis=0, concat_axis=1, tiled=True),
        lax.all_to_all(k2, "lon", split_axis=0, concat_axis=1, tiled=True),
        lax.all_to_all(v2, "lon", split_axis=0, concat_axis=1, tiled=True),
        lax.all_to_all(marks, "lon", split_axis=0, concat_axis=1, tiled=True),
    )
    row_out = row_attend(row_q, row_k, row_v, row_marks)
    o2 = lax.all_to_all(row_out, "lon", split_axis=1, concat_axis=0, tiled=True)
    return (
        y1.astype(jnp.float32) + jnp.dot(o2, w_out2, preferred_element_type=jnp.float32)
    ).astype(jnp.bfloat16)


def normed(af):
    mean = jnp.mean(af, -1, keepdims=True)
    diff = af - mean
    var = jnp.mean(diff * diff, -1, keepdims=True)
    return (diff * lax.rsqrt(var + EPS)).astype(jnp.bfloat16)


def mm(a, b):
    return jnp.dot(a, b, preferred_element_type=jnp.float32)


def pair_attend(q, k, v, bias, ocean_q, lane_a, ones):
    zero = jnp.zeros_like(k)
    kk = jnp.concatenate([jnp.where(lane_a, k, zero), jnp.where(lane_a, zero, k)], 0)
    s = lax.dot_general(q, kk, (((1,), (1,)), ((), ())), preferred_element_type=jnp.float32)
    fac = 1.4426950408889634 * 0.125
    probs = []
    for i in range(2):
        si = s[:, 128 * i : 128 * i + 128] + bias
        top = jnp.max(si, -1, keepdims=True)
        probs.append(jnp.exp2((si - top) * fac).astype(jnp.bfloat16))
    vv = jnp.concatenate([jnp.where(lane_a, v, zero), jnp.where(lane_a, zero, v)], 0)
    out = mm(jnp.concatenate(probs, 1), jnp.concatenate([vv, ones], 1))
    return (out[:, :128] * (ocean_q / (out[:, 128:] + (1.0 - ocean_q)))).astype(jnp.bfloat16)


D_ = 768
FLIPS = (4, 5, 6, 7, 2, 3, 1)

BASES = ((0, 0), (2, 6), (4, 2), (6, 4))
NEEDED = ((0, 0), (3, 6), (5, 3), (7, 5))
NEEDED_TOO = ((1, 1), (4, 7), (6, 4))


def flipped(index, flip):
    bits = [(index // 4) % 2, (index // 2) % 2, index % 2]
    total = 0
    for weight, bit in zip((4, 2, 1), bits):
        total = total + weight * ((1 - bit) if flip & weight else bit)
    return total


def band_kernel(
    x_ref, oc_ref, wq1, wk1, wv1, wo1, wq2, wk2, wv2, wo2, out_ref,
    x_buf, oc_out, oc_buf, win_buf, row_buf, w_buf, stage,
    y_ref, q_ref, k_ref, v_ref, q1_ref, k1_ref, v1_ref, o_ref,
    x_send, x_recv, oc_send, oc_recv, w_sem, z_send, z_recv,
):
    me = lax.axis_index("lon")
    mesh_id = pl.DeviceIdType.MESH
    peers = [flipped(me, flip) for flip in FLIPS]
    half, second = me // 4, (me // 2) % 2
    outer = (half + second + 1) % 2
    core = lax.axis_index("lat") % 2

    def pick(bit, there, other):
        return bit * flipped(me, there) + (1 - bit) * flipped(me, other)

    def by_core(pairs):
        first, then = pairs
        return [core * first + (1 - core) * then, core * then + (1 - core) * first]

    near = by_core([peers[4], peers[5]]) + [peers[6]]
    far = by_core([pick(outer, 4, 6), pick(outer, 5, 7)])
    far += by_core([pick(outer, 6, 4), pick(outer, 7, 5)])
    x_order = near + far
    z_order = peers

    def send_x(to, landing):
        return pltpu.make_async_remote_copy(
            x_ref.at[to], x_buf.at[landing], x_send, x_recv.at[landing],
            device_id={"lon": to}, device_id_type=mesh_id,
        )

    def send_oc(to, landing):
        return pltpu.make_async_remote_copy(
            oc_out.at[to], oc_buf.at[landing], oc_send, oc_recv,
            device_id={"lon": to}, device_id_type=mesh_id,
        )

    def send_z(to, landing, c):
        return pltpu.make_async_remote_copy(
            stage.at[to, c], out_ref.at[landing, c],
            z_send, z_recv,
            device_id={"lon": to}, device_id_type=mesh_id,
        )

    def own_z(c):
        return pltpu.make_async_copy(stage.at[me, c], out_ref.at[me, c], z_recv)

    def taken(ref, sem):
        pltpu.make_async_copy(ref, ref, sem).wait()

    own_x = pltpu.make_async_copy(x_ref.at[me], x_buf.at[me], x_recv.at[me])
    own_oc = pltpu.make_async_copy(oc_out.at[me], oc_buf.at[me], oc_recv)
    weights = [
        pltpu.make_async_copy(w, w_buf.at[i], w_sem)
        for i, w in enumerate((wq1, wk1, wv1, wo1, wq2, wk2, wv2, wo2))
    ]

    barrier = pltpu.get_barrier_semaphore()
    for to in peers:
        pl.semaphore_signal(barrier, inc=1, device_id={"lon": to}, device_id_type=mesh_id)
    own_x.start()
    oc_out[...] = oc_ref[...].astype(jnp.float32).T.reshape(8, 8, 16)
    own_oc.start()
    pl.semaphore_wait(barrier, 7)
    for to in peers:
        send_oc(to, me).start()
    for to in x_order:
        send_x(to, me).start()
    for copy in weights:
        copy.start()

    tok_q = lax.broadcasted_iota(jnp.int32, (128, 128), 0)
    tok_k = lax.broadcasted_iota(jnp.int32, (128, 128), 1)
    same = ((tok_q // 8) % 2) == ((tok_k // 8) % 2)
    eye = tok_q == tok_k
    lane_a = lax.broadcasted_iota(jnp.int32, (128, 128), 1) < 64
    one = lane_a.astype(jnp.float32)
    ones = jnp.concatenate([one, 1.0 - one], 0).astype(jnp.bfloat16)
    col = lax.broadcasted_iota(jnp.int32, (1, 16, 768), 1)

    taken(oc_buf, oc_recv)
    lane = lax.broadcasted_iota(jnp.int32, (8, 128), 1)
    sub = lax.broadcasted_iota(jnp.int32, (8, 128), 0)
    by_row = jnp.concatenate([oc_buf[g] for g in range(8)], 1)
    by_row = pltpu.roll(by_row, 124, 1)
    by_window = jnp.zeros((8, 128), jnp.float32)
    for d in range(8):
        turned = pltpu.roll(by_row, 16 * d, 1) if d else by_row
        turned = jnp.where(lane // 16 == sub, turned, 0.0)
        by_window = by_window + (pltpu.roll(turned, 8 - d, 0) if d else turned)
    win_buf[...] = by_window
    row_buf[...] = by_row
    taken(w_buf, w_sem)

    def column_of(row_vec):
        return jnp.sum(jnp.where(eye, row_vec, 0.0), 1, keepdims=True)

    def arrived(source):
        taken(x_buf.at[source], x_recv.at[source])

    late = 1 - second

    def in_turn(i, table):
        total = 4 * half
        for k, (a, b) in enumerate(table):
            total = total + jnp.where(i == k, (1 - late) * a + late * b, 0)
        return total % 8

    @pl.loop(0, 4)
    def _(i):
        first = in_turn(i, BASES)
        arrived(in_turn(i, NEEDED))

        @pl.when(i == 0)
        def _():
            arrived((4 * half + 2) % 8)

        @pl.when(i < 3)
        def _():
            arrived(in_turn(i, NEEDED_TOO))

        parts = []
        for g in range(3):
            block = x_buf[(first + g) % 8].astype(jnp.float32)
            parts.append(pltpu.roll(block, 12, 1))
        x = jnp.concatenate(
            [jnp.where(col < 12, parts[g], parts[g + 1]).reshape(128, D_) for g in range(2)], 0
        )
        h = normed(x)
        q1_ref[...] = mm(h, w_buf[0]).astype(jnp.bfloat16)
        k1_ref[...] = mm(h, w_buf[1]).astype(jnp.bfloat16)
        v1_ref[...] = mm(h, w_buf[2]).astype(jnp.bfloat16)
        for g in range(2):
            flags = win_buf[pl.ds((first + g) % 8, 1), :]
            bias = jnp.where(jnp.logical_and(same, flags > 0), 0.0, NEG)
            ocean_q = jnp.broadcast_to(column_of(flags), (128, 128))
            rows = slice(128 * g, 128 * g + 128)
            for p in range(6):
                lanes = slice(128 * p, 128 * p + 128)
                o_ref[rows, lanes] = pair_attend(
                    q1_ref[rows, lanes], k1_ref[rows, lanes], v1_ref[rows, lanes],
                    bias, ocean_q, lane_a, ones,
                )
        y = (x + mm(o_ref[...], w_buf[3])).astype(jnp.bfloat16)
        h2 = normed(y.astype(jnp.float32))
        for keep, value in (
            (y_ref, y),
            (q_ref, mm(h2, w_buf[4]).astype(jnp.bfloat16)),
            (k_ref, mm(h2, w_buf[5]).astype(jnp.bfloat16)),
            (v_ref, mm(h2, w_buf[6]).astype(jnp.bfloat16)),
        ):
            for g in range(2):
                keep[(first + g) % 8] = value[128 * g : 128 * g + 128].reshape(8, 16, D_)

    @pl.loop(0, 8)
    def _(r):
        flags = row_buf[pl.ds(r, 1), :]
        bias = jnp.where(flags > 0, 0.0, NEG)
        ocean_q = jnp.broadcast_to(column_of(flags), (128, 128))
        for p in range(6):
            lanes = slice(128 * p, 128 * p + 128)
            o_ref[:128, lanes] = pair_attend(
                q_ref[:, r, :, lanes].reshape(128, 128),
                k_ref[:, r, :, lanes].reshape(128, 128),
                v_ref[:, r, :, lanes].reshape(128, 128),
                bias, ocean_q, lane_a, ones,
            )
        z = mm(o_ref[:128, :], w_buf[7])
        zr = z.reshape(8, 16, D_) + y_ref[:, r].astype(jnp.float32)
        zr = pltpu.roll(zr, 4, 1)
        before = jnp.concatenate([zr[7:], zr[:7]], 0)
        stage[:, r] = jnp.where(col < 4, before, zr).astype(jnp.bfloat16)
        for to in z_order:
            send_z(to, me, r).start()
        own_z(r).start()

    taken(oc_buf.at[:7], oc_send)
    taken(x_buf.at[:7], x_send)
    taken(stage.at[:7], z_send)
    taken(out_ref, z_recv)


def on_bands(
    fields, ocean, w_query1, w_key1, w_value1, w_out1, w_query2, w_key2, w_value2, w_out2
):
    block = pltpu.VMEM((8, 8, 16, D_), jnp.bfloat16)
    part = pltpu.VMEM((256, D_), jnp.bfloat16)
    flags = pltpu.VMEM((8, 128), jnp.float32)
    sems = [(), (8,), (), (), (), (), ()]
    out = pl.pallas_call(
        band_kernel,
        out_shape=pltpu.VMEM((8, 8, 16, D_), jnp.bfloat16),
        in_specs=[pl.BlockSpec(memory_space=pltpu.HBM), pl.BlockSpec(memory_space=pltpu.VMEM)]
        + [pl.BlockSpec(memory_space=pltpu.HBM)] * 8,
        out_specs=pl.BlockSpec(memory_space=pl.ANY),
        scratch_shapes=[
            block,
            pltpu.VMEM((8, 8, 16), jnp.float32),
            pltpu.VMEM((8, 8, 16), jnp.float32),
            flags,
            flags,
            pltpu.VMEM((8, D_, D_), jnp.bfloat16),
            block,
        ]
        + [block] * 4
        + [part] * 4
        + [pltpu.SemaphoreType.DMA(shape) for shape in sems],
        compiler_params=pltpu.CompilerParams(
            vmem_limit_bytes=56 << 20, collective_id=0, has_side_effects=True
        ),
    )(
        fields.reshape(8, 8, 16, D_),
        ocean.T,
        w_query1, w_key1, w_value1, w_out1, w_query2, w_key2, w_value2, w_out2,
    )
    return out.reshape(64, 16, D_)


def solution(mesh):
    in_specs = (
        P(("grp", "lat"), "lon", None),
        P(("grp", "lat"), "lon"),
        P(),
        P(),
        P(),
        P(),
        P(),
        P(),
        P(),
        P(),
    )
    out_specs = P(("grp", "lat"), "lon", None)
    ranks = mesh.shape["lon"]

    def whole(fields, *rest):
        rows = fields.shape[0] // (mesh.shape["grp"] * mesh.shape["lat"])
        cols = fields.shape[1] // ranks
        banded = rows == 8 * ranks and cols == 16 and ranks == 8
        return jax.shard_map(
            on_bands if banded else on_device,
            mesh=mesh,
            in_specs=in_specs,
            out_specs=out_specs,
            check_vma=False,
        )(fields, *rest)

    return whole
```

```python
import jax
import jax.numpy as jnp
from jax import lax
from jax.experimental import pallas as pl
from jax.experimental.pallas import tpu as pltpu
from jax.sharding import PartitionSpec as P

HEADS = 12


EPS = 1e-05
NEG = -1e30


def passed_along(value, axis, steps):
    count = lax.axis_size(axis)
    pairs = [(source, (source + steps) % count) for source in range(count)]
    return lax.ppermute(value, axis, pairs)


def norm_rows(a):
    af = a.astype(jnp.float32)
    mean = jnp.mean(af, -1, keepdims=True)
    var = jnp.mean((af - mean) * (af - mean), -1, keepdims=True)
    return ((af - mean) * lax.rsqrt(var + EPS)).astype(jnp.bfloat16)


def project(h, weight):
    return jnp.dot(h, weight, preferred_element_type=jnp.float32).astype(jnp.bfloat16)


def masked_softmax(scores, key_ok, land_query):
    top = jnp.max(jnp.where(key_ok, scores, NEG), -1, keepdims=True)
    expo = jnp.where(key_ok, jnp.exp(scores - top), 0.0)
    total = jnp.sum(expo, -1, keepdims=True) + land_query[..., None]
    return (expo / total).astype(jnp.bfloat16)


def window_attend(query, keys, values, flags):
    rows, cols, width = query.shape
    nh = HEADS
    hd = width // nh
    scale = hd ** (-0.5)

    def tiles(a):
        a = a.reshape(rows // 8, 8, cols // 8, 8, nh, hd).transpose(0, 2, 4, 1, 3, 5)
        return a.reshape(rows // 8, cols // 8, nh, 64, hd)

    marks = (
        flags.reshape(rows // 8, 8, cols // 8, 8)
        .transpose(0, 2, 1, 3)
        .reshape(rows // 8, cols // 8, 64)
    )
    key_ok = (marks > 0)[:, :, None, None, :]
    land_query = (marks <= 0).astype(jnp.float32)[:, :, None, :]
    scores = (
        jnp.einsum(
            "abhqd,abhkd->abhqk", tiles(query), tiles(keys), preferred_element_type=jnp.float32
        )
        * scale
    )
    probs = masked_softmax(scores, key_ok, land_query)
    outs = jnp.einsum(
        "abhqk,abhkd->abhqd", probs, tiles(values), preferred_element_type=jnp.float32
    )
    outs = outs * (1.0 - land_query)[..., None]
    outs = outs.astype(jnp.bfloat16).reshape(rows // 8, cols // 8, nh, 8, 8, hd)
    return outs.transpose(0, 3, 1, 4, 2, 5).reshape(rows, cols, width)


def row_attend(query, keys, values, flags):
    rows, length, width = query.shape
    nh = HEADS
    hd = width // nh
    scale = hd ** (-0.5)
    key_ok = (flags > 0)[:, None, :]
    land_query = (flags <= 0).astype(jnp.float32)

    def head(index):
        qh = lax.dynamic_slice_in_dim(query, index * hd, hd, 2)
        kh = lax.dynamic_slice_in_dim(keys, index * hd, hd, 2)
        vh = lax.dynamic_slice_in_dim(values, index * hd, hd, 2)
        scores = jnp.einsum("rqd,rkd->rqk", qh, kh, preferred_element_type=jnp.float32) * scale
        probs = masked_softmax(scores, key_ok, land_query)
        return jnp.einsum("rqk,rkd->rqd", probs, vh, preferred_element_type=jnp.float32)

    outs = lax.map(head, jnp.arange(nh, dtype=jnp.int32))
    outs = outs.transpose(1, 2, 0, 3).reshape(rows, length, width)
    return (outs * (1.0 - land_query)[..., None]).astype(jnp.bfloat16)


def attend_columns(columns, marks, w_query1, w_key1, w_value1):
    return window_attend(
        project(columns, w_query1), project(columns, w_key1), project(columns, w_value1), marks
    )


def on_device(
    fields, ocean, w_query1, w_key1, w_value1, w_out1, w_query2, w_key2, w_value2, w_out2
):
    rows, cols, width = fields.shape
    normed = norm_rows(fields)
    marks = ocean.astype(jnp.bfloat16)
    edge_feats, edge_marks = passed_along((normed[:, cols - 4 :], marks[:, cols - 4 :]), "lon", 1)
    columns = jnp.concatenate([edge_feats, normed[:, : cols - 4]], 1)
    column_marks = jnp.concatenate([edge_marks, marks[:, : cols - 4]], 1)
    extended = attend_columns(columns, column_marks, w_query1, w_key1, w_value1)
    returned = passed_along(extended[:, :4], "lon", -1)
    o1 = jnp.concatenate([extended[:, 4:], returned], 1)
    y1 = (
        fields.astype(jnp.float32) + jnp.dot(o1, w_out1, preferred_element_type=jnp.float32)
    ).astype(jnp.bfloat16)
    h2 = norm_rows(y1)
    q2 = project(h2, w_query2)
    k2 = project(h2, w_key2)
    v2 = project(h2, w_value2)
    row_q, row_k, row_v, row_marks = (
        lax.all_to_all(q2, "lon", split_axis=0, concat_axis=1, tiled=True),
        lax.all_to_all(k2, "lon", split_axis=0, concat_axis=1, tiled=True),
        lax.all_to_all(v2, "lon", split_axis=0, concat_axis=1, tiled=True),
        lax.all_to_all(marks, "lon", split_axis=0, concat_axis=1, tiled=True),
    )
    row_out = row_attend(row_q, row_k, row_v, row_marks)
    o2 = lax.all_to_all(row_out, "lon", split_axis=1, concat_axis=0, tiled=True)
    return (
        y1.astype(jnp.float32) + jnp.dot(o2, w_out2, preferred_element_type=jnp.float32)
    ).astype(jnp.bfloat16)


def normed(af):
    mean = jnp.mean(af, -1, keepdims=True)
    diff = af - mean
    var = jnp.mean(diff * diff, -1, keepdims=True)
    return (diff * lax.rsqrt(var + EPS)).astype(jnp.bfloat16)


def mm(a, b):
    return jnp.dot(a, b, preferred_element_type=jnp.float32)


def pair_attend(q, k, v, bias, ocean_q, lane_a, ones):
    zero = jnp.zeros_like(k)
    kk = jnp.concatenate([jnp.where(lane_a, k, zero), jnp.where(lane_a, zero, k)], 0)
    s = lax.dot_general(q, kk, (((1,), (1,)), ((), ())), preferred_element_type=jnp.float32)
    fac = 1.4426950408889634 * 0.125
    probs = []
    for i in range(2):
        si = s[:, 128 * i : 128 * i + 128] + bias
        top = jnp.max(si, -1, keepdims=True)
        probs.append(jnp.exp2((si - top) * fac).astype(jnp.bfloat16))
    vv = jnp.concatenate([jnp.where(lane_a, v, zero), jnp.where(lane_a, zero, v)], 0)
    out = mm(jnp.concatenate(probs, 1), jnp.concatenate([vv, ones], 1))
    return (out[:, :128] * (ocean_q / (out[:, 128:] + (1.0 - ocean_q)))).astype(jnp.bfloat16)


D_ = 768
FLIPS = (4, 5, 6, 7, 2, 3, 1)

TURNS = (
    (0, 6, 2, 4), (1, 7, 5, 3), (0, 2, 6, 4), (1, 7, 5, 3),
    (0, 2, 4, 6), (1, 7, 3, 5), (0, 2, 4, 6), (1, 3, 7, 5),
)


def plan():
    bases, needs = [], []
    for rank, turns in enumerate(TURNS):
        seen, missing = set(), []
        for base in turns:
            fresh = [(base + k) % 8 for k in range(3) if (base + k) % 8 not in seen]
            seen.update(fresh)
            missing.append([(block + 4 * (rank // 4)) % 8 for block in fresh])
        bases.append([(base + 4 * (rank // 4)) % 8 for base in turns])
        needs.append(missing)
    return bases, needs


def flipped(index, flip):
    bits = [(index // 4) % 2, (index // 2) % 2, index % 2]
    total = 0
    for weight, bit in zip((4, 2, 1), bits):
        total = total + weight * ((1 - bit) if flip & weight else bit)
    return total


def band_kernel(
    x_ref, oc_ref, wq1, wk1, wv1, wo1, wq2, wk2, wv2, wo2, out_ref,
    x_buf, oc_out, oc_buf, win_buf, row_buf, w_buf, stage,
    y_ref, q_ref, k_ref, v_ref, q1_ref, k1_ref, v1_ref, o_ref,
    x_send, x_recv, oc_send, oc_recv, w_sem, z_send, z_recv,
):
    me = lax.axis_index("lon")
    mesh_id = pl.DeviceIdType.MESH
    peers = [flipped(me, flip) for flip in FLIPS]
    half, second = me // 4, (me // 2) % 2
    outer = (half + second + 1) % 2

    def pick(there, other):
        return outer * flipped(me, there) + (1 - outer) * flipped(me, other)

    far = [pick(4, 6), pick(5, 7), pick(6, 4), pick(7, 5)]
    x_order = [pick(3, 2), pick(2, 3), peers[6]] + far
    z_order = peers

    def send_x(to, landing):
        return pltpu.make_async_remote_copy(
            x_ref.at[to], x_buf.at[landing], x_send, x_recv.at[landing],
            device_id={"lon": to}, device_id_type=mesh_id,
        )

    def send_oc(to, landing):
        return pltpu.make_async_remote_copy(
            oc_out.at[to], oc_buf.at[landing], oc_send, oc_recv,
            device_id={"lon": to}, device_id_type=mesh_id,
        )

    def send_z(to, landing, c):
        return pltpu.make_async_remote_copy(
            stage.at[to, c], out_ref.at[landing, c],
            z_send, z_recv,
            device_id={"lon": to}, device_id_type=mesh_id,
        )

    def own_z(c):
        return pltpu.make_async_copy(stage.at[me, c], out_ref.at[me, c], z_recv)

    def taken(ref, sem):
        pltpu.make_async_copy(ref, ref, sem).wait()

    own_x = pltpu.make_async_copy(x_ref.at[me], x_buf.at[me], x_recv.at[me])
    own_oc = pltpu.make_async_copy(oc_out.at[me], oc_buf.at[me], oc_recv)
    weights = [
        pltpu.make_async_copy(w, w_buf.at[i], w_sem)
        for i, w in enumerate((wq1, wk1, wv1, wo1, wq2, wk2, wv2, wo2))
    ]

    barrier = pltpu.get_barrier_semaphore()
    for to in peers:
        pl.semaphore_signal(barrier, inc=1, device_id={"lon": to}, device_id_type=mesh_id)
    own_x.start()
    oc_out[...] = oc_ref[...].astype(jnp.float32).T.reshape(8, 8, 16)
    own_oc.start()
    pl.semaphore_wait(barrier, 7)
    for to in peers:
        send_oc(to, me).start()
    for to in x_order:
        send_x(to, me).start()
    for copy in weights:
        copy.start()

    tok_q = lax.broadcasted_iota(jnp.int32, (128, 128), 0)
    tok_k = lax.broadcasted_iota(jnp.int32, (128, 128), 1)
    same = ((tok_q // 8) % 2) == ((tok_k // 8) % 2)
    eye = tok_q == tok_k
    lane_a = lax.broadcasted_iota(jnp.int32, (128, 128), 1) < 64
    one = lane_a.astype(jnp.float32)
    ones = jnp.concatenate([one, 1.0 - one], 0).astype(jnp.bfloat16)
    col = lax.broadcasted_iota(jnp.int32, (1, 16, 768), 1)

    taken(oc_buf, oc_recv)
    lane = lax.broadcasted_iota(jnp.int32, (8, 128), 1)
    sub = lax.broadcasted_iota(jnp.int32, (8, 128), 0)
    by_row = jnp.concatenate([oc_buf[g] for g in range(8)], 1)
    by_row = pltpu.roll(by_row, 124, 1)
    by_window = jnp.zeros((8, 128), jnp.float32)
    for d in range(8):
        turned = pltpu.roll(by_row, 16 * d, 1) if d else by_row
        turned = jnp.where(lane // 16 == sub, turned, 0.0)
        by_window = by_window + (pltpu.roll(turned, 8 - d, 0) if d else turned)
    win_buf[...] = by_window
    row_buf[...] = by_row
    taken(w_buf, w_sem)

    def column_of(row_vec):
        return jnp.sum(jnp.where(eye, row_vec, 0.0), 1, keepdims=True)

    def arrived(source):
        taken(x_buf.at[source], x_recv.at[source])

    bases, needs = plan()

    def by_rank(values):
        total = 0
        for rank, value in enumerate(values):
            total = total + jnp.where(me == rank, value, 0)
        return total

    base_of = [by_rank([bases[rank][turn] for rank in range(8)]) for turn in range(4)]
    need_of = [
        [by_rank([needs[rank][turn][k] for rank in range(8)]) for k in range(count)]
        for turn, count in enumerate((3, 2, 2, 1))
    ]

    @pl.loop(0, 4)
    def _(i):
        def at_turn(values):
            total = 0
            for turn, value in enumerate(values):
                total = total + jnp.where(i == turn, value, 0)
            return total

        first = at_turn(base_of)
        arrived(at_turn([need[0] for need in need_of]))

        @pl.when(i == 0)
        def _():
            arrived(need_of[0][2])

        @pl.when(i < 3)
        def _():
            arrived(at_turn([need[1] for need in need_of[:3]]))

        parts = []
        for g in range(3):
            block = x_buf[(first + g) % 8].astype(jnp.float32)
            parts.append(pltpu.roll(block, 12, 1))
        x = jnp.concatenate(
            [jnp.where(col < 12, parts[g], parts[g + 1]).reshape(128, D_) for g in range(2)], 0
        )
        h = normed(x)
        q1_ref[...] = mm(h, w_buf[0]).astype(jnp.bfloat16)
        k1_ref[...] = mm(h, w_buf[1]).astype(jnp.bfloat16)
        v1_ref[...] = mm(h, w_buf[2]).astype(jnp.bfloat16)
        for g in range(2):
            flags = win_buf[pl.ds((first + g) % 8, 1), :]
            bias = jnp.where(jnp.logical_and(same, flags > 0), 0.0, NEG)
            ocean_q = jnp.broadcast_to(column_of(flags), (128, 128))
            rows = slice(128 * g, 128 * g + 128)
            for p in range(6):
                lanes = slice(128 * p, 128 * p + 128)
                o_ref[rows, lanes] = pair_attend(
                    q1_ref[rows, lanes], k1_ref[rows, lanes], v1_ref[rows, lanes],
                    bias, ocean_q, lane_a, ones,
                )
        y = (x + mm(o_ref[...], w_buf[3])).astype(jnp.bfloat16)
        h2 = normed(y.astype(jnp.float32))
        for keep, value in (
            (y_ref, y),
            (q_ref, mm(h2, w_buf[4]).astype(jnp.bfloat16)),
            (k_ref, mm(h2, w_buf[5]).astype(jnp.bfloat16)),
            (v_ref, mm(h2, w_buf[6]).astype(jnp.bfloat16)),
        ):
            for g in range(2):
                keep[(first + g) % 8] = value[128 * g : 128 * g + 128].reshape(8, 16, D_)

    @pl.loop(0, 8)
    def _(r):
        flags = row_buf[pl.ds(r, 1), :]
        bias = jnp.where(flags > 0, 0.0, NEG)
        ocean_q = jnp.broadcast_to(column_of(flags), (128, 128))
        for p in range(6):
            lanes = slice(128 * p, 128 * p + 128)
            o_ref[:128, lanes] = pair_attend(
                q_ref[:, r, :, lanes].reshape(128, 128),
                k_ref[:, r, :, lanes].reshape(128, 128),
                v_ref[:, r, :, lanes].reshape(128, 128),
                bias, ocean_q, lane_a, ones,
            )
        z = mm(o_ref[:128, :], w_buf[7])
        zr = z.reshape(8, 16, D_) + y_ref[:, r].astype(jnp.float32)
        zr = pltpu.roll(zr, 4, 1)
        before = jnp.concatenate([zr[7:], zr[:7]], 0)
        stage[:, r] = jnp.where(col < 4, before, zr).astype(jnp.bfloat16)
        for to in z_order:
            send_z(to, me, r).start()
        own_z(r).start()

    taken(oc_buf.at[:7], oc_send)
    taken(x_buf.at[:7], x_send)
    taken(stage.at[:7], z_send)
    taken(out_ref, z_recv)


def on_bands(
    fields, ocean, w_query1, w_key1, w_value1, w_out1, w_query2, w_key2, w_value2, w_out2
):
    block = pltpu.VMEM((8, 8, 16, D_), jnp.bfloat16)
    part = pltpu.VMEM((256, D_), jnp.bfloat16)
    flags = pltpu.VMEM((8, 128), jnp.float32)
    sems = [(), (8,), (), (), (), (), ()]
    out = pl.pallas_call(
        band_kernel,
        out_shape=pltpu.VMEM((8, 8, 16, D_), jnp.bfloat16),
        in_specs=[pl.BlockSpec(memory_space=pltpu.HBM), pl.BlockSpec(memory_space=pltpu.VMEM)]
        + [pl.BlockSpec(memory_space=pltpu.HBM)] * 8,
        out_specs=pl.BlockSpec(memory_space=pl.ANY),
        scratch_shapes=[
            block,
            pltpu.VMEM((8, 8, 16), jnp.float32),
            pltpu.VMEM((8, 8, 16), jnp.float32),
            flags,
            flags,
            pltpu.VMEM((8, D_, D_), jnp.bfloat16),
            block,
        ]
        + [block] * 4
        + [part] * 4
        + [pltpu.SemaphoreType.DMA(shape) for shape in sems],
        compiler_params=pltpu.CompilerParams(
            vmem_limit_bytes=56 << 20, collective_id=0, has_side_effects=True
        ),
    )(
        fields.reshape(8, 8, 16, D_),
        ocean.T,
        w_query1, w_key1, w_value1, w_out1, w_query2, w_key2, w_value2, w_out2,
    )
    return out.reshape(64, 16, D_)


def solution(mesh):
    in_specs = (
        P(("grp", "lat"), "lon", None),
        P(("grp", "lat"), "lon"),
        P(),
        P(),
        P(),
        P(),
        P(),
        P(),
        P(),
        P(),
    )
    out_specs = P(("grp", "lat"), "lon", None)
    ranks = mesh.shape["lon"]

    def whole(fields, *rest):
        rows = fields.shape[0] // (mesh.shape["grp"] * mesh.shape["lat"])
        cols = fields.shape[1] // ranks
        banded = rows == 8 * ranks and cols == 16 and ranks == 8
        return jax.shard_map(
            on_bands if banded else on_device,
            mesh=mesh,
            in_specs=in_specs,
            out_specs=out_specs,
            check_vma=False,
        )(fields, *rest)

    return whole
```

```python
import jax
import jax.numpy as jnp
from jax import lax
from jax.experimental import pallas as pl
from jax.experimental.pallas import tpu as pltpu
from jax.sharding import PartitionSpec as P

HEADS = 12


EPS = 1e-05
NEG = -1e30


def passed_along(value, axis, steps):
    count = lax.axis_size(axis)
    pairs = [(source, (source + steps) % count) for source in range(count)]
    return lax.ppermute(value, axis, pairs)


def norm_rows(a):
    af = a.astype(jnp.float32)
    mean = jnp.mean(af, -1, keepdims=True)
    var = jnp.mean((af - mean) * (af - mean), -1, keepdims=True)
    return ((af - mean) * lax.rsqrt(var + EPS)).astype(jnp.bfloat16)


def project(h, weight):
    return jnp.dot(h, weight, preferred_element_type=jnp.float32).astype(jnp.bfloat16)


def masked_softmax(scores, key_ok, land_query):
    top = jnp.max(jnp.where(key_ok, scores, NEG), -1, keepdims=True)
    expo = jnp.where(key_ok, jnp.exp(scores - top), 0.0)
    total = jnp.sum(expo, -1, keepdims=True) + land_query[..., None]
    return (expo / total).astype(jnp.bfloat16)


def window_attend(query, keys, values, flags):
    rows, cols, width = query.shape
    nh = HEADS
    hd = width // nh
    scale = hd ** (-0.5)

    def tiles(a):
        a = a.reshape(rows // 8, 8, cols // 8, 8, nh, hd).transpose(0, 2, 4, 1, 3, 5)
        return a.reshape(rows // 8, cols // 8, nh, 64, hd)

    marks = (
        flags.reshape(rows // 8, 8, cols // 8, 8)
        .transpose(0, 2, 1, 3)
        .reshape(rows // 8, cols // 8, 64)
    )
    key_ok = (marks > 0)[:, :, None, None, :]
    land_query = (marks <= 0).astype(jnp.float32)[:, :, None, :]
    scores = (
        jnp.einsum(
            "abhqd,abhkd->abhqk", tiles(query), tiles(keys), preferred_element_type=jnp.float32
        )
        * scale
    )
    probs = masked_softmax(scores, key_ok, land_query)
    outs = jnp.einsum(
        "abhqk,abhkd->abhqd", probs, tiles(values), preferred_element_type=jnp.float32
    )
    outs = outs * (1.0 - land_query)[..., None]
    outs = outs.astype(jnp.bfloat16).reshape(rows // 8, cols // 8, nh, 8, 8, hd)
    return outs.transpose(0, 3, 1, 4, 2, 5).reshape(rows, cols, width)


def row_attend(query, keys, values, flags):
    rows, length, width = query.shape
    nh = HEADS
    hd = width // nh
    scale = hd ** (-0.5)
    key_ok = (flags > 0)[:, None, :]
    land_query = (flags <= 0).astype(jnp.float32)

    def head(index):
        qh = lax.dynamic_slice_in_dim(query, index * hd, hd, 2)
        kh = lax.dynamic_slice_in_dim(keys, index * hd, hd, 2)
        vh = lax.dynamic_slice_in_dim(values, index * hd, hd, 2)
        scores = jnp.einsum("rqd,rkd->rqk", qh, kh, preferred_element_type=jnp.float32) * scale
        probs = masked_softmax(scores, key_ok, land_query)
        return jnp.einsum("rqk,rkd->rqd", probs, vh, preferred_element_type=jnp.float32)

    outs = lax.map(head, jnp.arange(nh, dtype=jnp.int32))
    outs = outs.transpose(1, 2, 0, 3).reshape(rows, length, width)
    return (outs * (1.0 - land_query)[..., None]).astype(jnp.bfloat16)


def attend_columns(columns, marks, w_query1, w_key1, w_value1):
    return window_attend(
        project(columns, w_query1), project(columns, w_key1), project(columns, w_value1), marks
    )


def on_device(
    fields, ocean, w_query1, w_key1, w_value1, w_out1, w_query2, w_key2, w_value2, w_out2
):
    rows, cols, width = fields.shape
    normed = norm_rows(fields)
    marks = ocean.astype(jnp.bfloat16)
    edge_feats, edge_marks = passed_along((normed[:, cols - 4 :], marks[:, cols - 4 :]), "lon", 1)
    columns = jnp.concatenate([edge_feats, normed[:, : cols - 4]], 1)
    column_marks = jnp.concatenate([edge_marks, marks[:, : cols - 4]], 1)
    extended = attend_columns(columns, column_marks, w_query1, w_key1, w_value1)
    returned = passed_along(extended[:, :4], "lon", -1)
    o1 = jnp.concatenate([extended[:, 4:], returned], 1)
    y1 = (
        fields.astype(jnp.float32) + jnp.dot(o1, w_out1, preferred_element_type=jnp.float32)
    ).astype(jnp.bfloat16)
    h2 = norm_rows(y1)
    q2 = project(h2, w_query2)
    k2 = project(h2, w_key2)
    v2 = project(h2, w_value2)
    row_q, row_k, row_v, row_marks = (
        lax.all_to_all(q2, "lon", split_axis=0, concat_axis=1, tiled=True),
        lax.all_to_all(k2, "lon", split_axis=0, concat_axis=1, tiled=True),
        lax.all_to_all(v2, "lon", split_axis=0, concat_axis=1, tiled=True),
        lax.all_to_all(marks, "lon", split_axis=0, concat_axis=1, tiled=True),
    )
    row_out = row_attend(row_q, row_k, row_v, row_marks)
    o2 = lax.all_to_all(row_out, "lon", split_axis=1, concat_axis=0, tiled=True)
    return (
        y1.astype(jnp.float32) + jnp.dot(o2, w_out2, preferred_element_type=jnp.float32)
    ).astype(jnp.bfloat16)


def normed(af):
    mean = jnp.mean(af, -1, keepdims=True)
    diff = af - mean
    var = jnp.mean(diff * diff, -1, keepdims=True)
    return (diff * lax.rsqrt(var + EPS)).astype(jnp.bfloat16)


def mm(a, b):
    return jnp.dot(a, b, preferred_element_type=jnp.float32)


def pair_attend(q, k, v, bias, ocean_q, lane_a, ones):
    zero = jnp.zeros_like(k)
    kk = jnp.concatenate([jnp.where(lane_a, k, zero), jnp.where(lane_a, zero, k)], 0)
    s = lax.dot_general(q, kk, (((1,), (1,)), ((), ())), preferred_element_type=jnp.float32)
    fac = 1.4426950408889634 * 0.125
    probs = []
    for i in range(2):
        si = s[:, 128 * i : 128 * i + 128] + bias
        top = jnp.max(si, -1, keepdims=True)
        probs.append(jnp.exp2((si - top) * fac).astype(jnp.bfloat16))
    vv = jnp.concatenate([jnp.where(lane_a, v, zero), jnp.where(lane_a, zero, v)], 0)
    out = mm(jnp.concatenate(probs, 1), jnp.concatenate([vv, ones], 1))
    return (out[:, :128] * (ocean_q / (out[:, 128:] + (1.0 - ocean_q)))).astype(jnp.bfloat16)


D_ = 768
FLIPS = (4, 5, 6, 7, 2, 3, 1)

TURNS = (
    (0, 6, 2, 4), (1, 7, 5, 3), (0, 2, 6, 4), (1, 7, 5, 3),
    (0, 2, 4, 6), (1, 7, 3, 5), (0, 2, 4, 6), (1, 3, 7, 5),
)


def plan():
    bases, needs = [], []
    for rank, turns in enumerate(TURNS):
        seen, missing = set(), []
        for base in turns:
            fresh = [(base + k) % 8 for k in range(3) if (base + k) % 8 not in seen]
            seen.update(fresh)
            missing.append([(block + 4 * (rank // 4)) % 8 for block in fresh])
        bases.append([(base + 4 * (rank // 4)) % 8 for base in turns])
        needs.append(missing)
    return bases, needs


def flipped(index, flip):
    bits = [(index // 4) % 2, (index // 2) % 2, index % 2]
    total = 0
    for weight, bit in zip((4, 2, 1), bits):
        total = total + weight * ((1 - bit) if flip & weight else bit)
    return total


def band_kernel(
    x_ref, oc_ref, wq1, wk1, wv1, wo1, wq2, wk2, wv2, wo2, out_ref,
    x_buf, oc_out, oc_buf, win_buf, row_buf, w_buf, stage,
    y_ref, q_ref, k_ref, v_ref, q1_ref, k1_ref, v1_ref, o_ref,
    x_send, x_recv, oc_send, oc_recv, w_sem, z_send, z_recv,
):
    me = lax.axis_index("lon")
    mesh_id = pl.DeviceIdType.MESH
    peers = [flipped(me, flip) for flip in FLIPS]
    half, second = me // 4, (me // 2) % 2
    outer = (half + second + 1) % 2

    def pick(there, other):
        return outer * flipped(me, there) + (1 - outer) * flipped(me, other)

    far = [pick(4, 6), pick(5, 7), pick(6, 4), pick(7, 5)]
    x_order = [pick(3, 2), pick(2, 3), peers[6]] + far

    def ends(there, other):
        return (1 - second) * flipped(me, there) + second * flipped(me, other)

    soon = [ends(4, 6), ends(5, 7)]
    later = [ends(6, 4), ends(7, 5)]

    def send_x(to, landing):
        return pltpu.make_async_remote_copy(
            x_ref.at[to], x_buf.at[landing], x_send, x_recv.at[landing],
            device_id={"lon": to}, device_id_type=mesh_id,
        )

    def send_oc(to, landing):
        return pltpu.make_async_remote_copy(
            oc_out.at[to], oc_buf.at[landing], oc_send, oc_recv,
            device_id={"lon": to}, device_id_type=mesh_id,
        )

    def send_z(to, landing, c, count):
        return pltpu.make_async_remote_copy(
            stage.at[to, pl.ds(c, count)], out_ref.at[landing, pl.ds(c, count)],
            z_send, z_recv,
            device_id={"lon": to}, device_id_type=mesh_id,
        )

    def own_z(c):
        return pltpu.make_async_copy(stage.at[me, c], out_ref.at[me, c], z_recv)

    def taken(ref, sem):
        pltpu.make_async_copy(ref, ref, sem).wait()

    own_x = pltpu.make_async_copy(x_ref.at[me], x_buf.at[me], x_recv.at[me])
    own_oc = pltpu.make_async_copy(oc_out.at[me], oc_buf.at[me], oc_recv)
    weights = [
        pltpu.make_async_copy(w, w_buf.at[i], w_sem)
        for i, w in enumerate((wq1, wk1, wv1, wo1, wq2, wk2, wv2, wo2))
    ]

    barrier = pltpu.get_barrier_semaphore()
    for to in peers:
        pl.semaphore_signal(barrier, inc=1, device_id={"lon": to}, device_id_type=mesh_id)
    own_x.start()
    oc_out[...] = oc_ref[...].astype(jnp.float32).T.reshape(8, 8, 16)
    own_oc.start()
    pl.semaphore_wait(barrier, 7)
    for to in peers:
        send_oc(to, me).start()
    for to in x_order:
        send_x(to, me).start()
    for copy in weights:
        copy.start()

    tok_q = lax.broadcasted_iota(jnp.int32, (128, 128), 0)
    tok_k = lax.broadcasted_iota(jnp.int32, (128, 128), 1)
    same = ((tok_q // 8) % 2) == ((tok_k // 8) % 2)
    eye = tok_q == tok_k
    lane_a = lax.broadcasted_iota(jnp.int32, (128, 128), 1) < 64
    one = lane_a.astype(jnp.float32)
    ones = jnp.concatenate([one, 1.0 - one], 0).astype(jnp.bfloat16)
    col = lax.broadcasted_iota(jnp.int32, (1, 16, 768), 1)

    taken(oc_buf, oc_recv)
    lane = lax.broadcasted_iota(jnp.int32, (8, 128), 1)
    sub = lax.broadcasted_iota(jnp.int32, (8, 128), 0)
    by_row = jnp.concatenate([oc_buf[g] for g in range(8)], 1)
    by_row = pltpu.roll(by_row, 124, 1)
    by_window = jnp.zeros((8, 128), jnp.float32)
    for d in range(8):
        turned = pltpu.roll(by_row, 16 * d, 1) if d else by_row
        turned = jnp.where(lane // 16 == sub, turned, 0.0)
        by_window = by_window + (pltpu.roll(turned, 8 - d, 0) if d else turned)
    win_buf[...] = by_window
    row_buf[...] = by_row
    taken(w_buf, w_sem)

    def column_of(row_vec):
        return jnp.sum(jnp.where(eye, row_vec, 0.0), 1, keepdims=True)

    def arrived(source):
        taken(x_buf.at[source], x_recv.at[source])

    bases, needs = plan()

    def by_rank(values):
        total = 0
        for rank, value in enumerate(values):
            total = total + jnp.where(me == rank, value, 0)
        return total

    base_of = [by_rank([bases[rank][turn] for rank in range(8)]) for turn in range(4)]
    need_of = [
        [by_rank([needs[rank][turn][k] for rank in range(8)]) for k in range(count)]
        for turn, count in enumerate((3, 2, 2, 1))
    ]

    @pl.loop(0, 4)
    def _(i):
        def at_turn(values):
            total = 0
            for turn, value in enumerate(values):
                total = total + jnp.where(i == turn, value, 0)
            return total

        first = at_turn(base_of)
        arrived(at_turn([need[0] for need in need_of]))

        @pl.when(i == 0)
        def _():
            arrived(need_of[0][2])

        @pl.when(i < 3)
        def _():
            arrived(at_turn([need[1] for need in need_of[:3]]))

        parts = []
        for g in range(3):
            block = x_buf[(first + g) % 8].astype(jnp.float32)
            parts.append(pltpu.roll(block, 12, 1))
        x = jnp.concatenate(
            [jnp.where(col < 12, parts[g], parts[g + 1]).reshape(128, D_) for g in range(2)], 0
        )
        h = normed(x)
        q1_ref[...] = mm(h, w_buf[0]).astype(jnp.bfloat16)
        k1_ref[...] = mm(h, w_buf[1]).astype(jnp.bfloat16)
        v1_ref[...] = mm(h, w_buf[2]).astype(jnp.bfloat16)
        for g in range(2):
            flags = win_buf[pl.ds((first + g) % 8, 1), :]
            bias = jnp.where(jnp.logical_and(same, flags > 0), 0.0, NEG)
            ocean_q = jnp.broadcast_to(column_of(flags), (128, 128))
            rows = slice(128 * g, 128 * g + 128)
            for p in range(6):
                lanes = slice(128 * p, 128 * p + 128)
                o_ref[rows, lanes] = pair_attend(
                    q1_ref[rows, lanes], k1_ref[rows, lanes], v1_ref[rows, lanes],
                    bias, ocean_q, lane_a, ones,
                )
        y = (x + mm(o_ref[...], w_buf[3])).astype(jnp.bfloat16)
        h2 = normed(y.astype(jnp.float32))
        for keep, value in (
            (y_ref, y),
            (q_ref, mm(h2, w_buf[4]).astype(jnp.bfloat16)),
            (k_ref, mm(h2, w_buf[5]).astype(jnp.bfloat16)),
            (v_ref, mm(h2, w_buf[6]).astype(jnp.bfloat16)),
        ):
            for g in range(2):
                keep[(first + g) % 8] = value[128 * g : 128 * g + 128].reshape(8, 16, D_)

    @pl.loop(0, 8)
    def _(r):
        flags = row_buf[pl.ds(r, 1), :]
        bias = jnp.where(flags > 0, 0.0, NEG)
        ocean_q = jnp.broadcast_to(column_of(flags), (128, 128))
        for p in range(6):
            lanes = slice(128 * p, 128 * p + 128)
            o_ref[:128, lanes] = pair_attend(
                q_ref[:, r, :, lanes].reshape(128, 128),
                k_ref[:, r, :, lanes].reshape(128, 128),
                v_ref[:, r, :, lanes].reshape(128, 128),
                bias, ocean_q, lane_a, ones,
            )
        z = mm(o_ref[:128, :], w_buf[7])
        zr = z.reshape(8, 16, D_) + y_ref[:, r].astype(jnp.float32)
        zr = pltpu.roll(zr, 4, 1)
        before = jnp.concatenate([zr[7:], zr[:7]], 0)
        stage[:, r] = jnp.where(col < 4, before, zr).astype(jnp.bfloat16)
        for to in soon + peers[4:]:
            send_z(to, me, r, 1).start()
        own_z(r).start()

    for to in later:
        send_z(to, me, 0, 8).start()

    taken(oc_buf.at[:7], oc_send)
    taken(x_buf.at[:7], x_send)
    taken(stage.at[:7], z_send)
    taken(out_ref, z_recv)


def on_bands(
    fields, ocean, w_query1, w_key1, w_value1, w_out1, w_query2, w_key2, w_value2, w_out2
):
    block = pltpu.VMEM((8, 8, 16, D_), jnp.bfloat16)
    part = pltpu.VMEM((256, D_), jnp.bfloat16)
    flags = pltpu.VMEM((8, 128), jnp.float32)
    sems = [(), (8,), (), (), (), (), ()]
    out = pl.pallas_call(
        band_kernel,
        out_shape=pltpu.VMEM((8, 8, 16, D_), jnp.bfloat16),
        in_specs=[pl.BlockSpec(memory_space=pltpu.HBM), pl.BlockSpec(memory_space=pltpu.VMEM)]
        + [pl.BlockSpec(memory_space=pltpu.HBM)] * 8,
        out_specs=pl.BlockSpec(memory_space=pl.ANY),
        scratch_shapes=[
            block,
            pltpu.VMEM((8, 8, 16), jnp.float32),
            pltpu.VMEM((8, 8, 16), jnp.float32),
            flags,
            flags,
            pltpu.VMEM((8, D_, D_), jnp.bfloat16),
            block,
        ]
        + [block] * 4
        + [part] * 4
        + [pltpu.SemaphoreType.DMA(shape) for shape in sems],
        compiler_params=pltpu.CompilerParams(
            vmem_limit_bytes=56 << 20, collective_id=0, has_side_effects=True
        ),
    )(
        fields.reshape(8, 8, 16, D_),
        ocean.T,
        w_query1, w_key1, w_value1, w_out1, w_query2, w_key2, w_value2, w_out2,
    )
    return out.reshape(64, 16, D_)


def solution(mesh):
    in_specs = (
        P(("grp", "lat"), "lon", None),
        P(("grp", "lat"), "lon"),
        P(),
        P(),
        P(),
        P(),
        P(),
        P(),
        P(),
        P(),
    )
    out_specs = P(("grp", "lat"), "lon", None)
    ranks = mesh.shape["lon"]

    def whole(fields, *rest):
        rows = fields.shape[0] // (mesh.shape["grp"] * mesh.shape["lat"])
        cols = fields.shape[1] // ranks
        banded = rows == 8 * ranks and cols == 16 and ranks == 8
        return jax.shard_map(
            on_bands if banded else on_device,
            mesh=mesh,
            in_specs=in_specs,
            out_specs=out_specs,
            check_vma=False,
        )(fields, *rest)

    return whole
```

```python
import jax
import jax.numpy as jnp
from jax import lax
from jax.experimental import pallas as pl
from jax.experimental.pallas import tpu as pltpu
from jax.sharding import PartitionSpec as P

HEADS = 12


EPS = 1e-05
NEG = -1e30


def passed_along(value, axis, steps):
    count = lax.axis_size(axis)
    pairs = [(source, (source + steps) % count) for source in range(count)]
    return lax.ppermute(value, axis, pairs)


def norm_rows(a):
    af = a.astype(jnp.float32)
    mean = jnp.mean(af, -1, keepdims=True)
    var = jnp.mean((af - mean) * (af - mean), -1, keepdims=True)
    return ((af - mean) * lax.rsqrt(var + EPS)).astype(jnp.bfloat16)


def project(h, weight):
    return jnp.dot(h, weight, preferred_element_type=jnp.float32).astype(jnp.bfloat16)


def masked_softmax(scores, key_ok, land_query):
    top = jnp.max(jnp.where(key_ok, scores, NEG), -1, keepdims=True)
    expo = jnp.where(key_ok, jnp.exp(scores - top), 0.0)
    total = jnp.sum(expo, -1, keepdims=True) + land_query[..., None]
    return (expo / total).astype(jnp.bfloat16)


def window_attend(query, keys, values, flags):
    rows, cols, width = query.shape
    nh = HEADS
    hd = width // nh
    scale = hd ** (-0.5)

    def tiles(a):
        a = a.reshape(rows // 8, 8, cols // 8, 8, nh, hd).transpose(0, 2, 4, 1, 3, 5)
        return a.reshape(rows // 8, cols // 8, nh, 64, hd)

    marks = (
        flags.reshape(rows // 8, 8, cols // 8, 8)
        .transpose(0, 2, 1, 3)
        .reshape(rows // 8, cols // 8, 64)
    )
    key_ok = (marks > 0)[:, :, None, None, :]
    land_query = (marks <= 0).astype(jnp.float32)[:, :, None, :]
    scores = (
        jnp.einsum(
            "abhqd,abhkd->abhqk", tiles(query), tiles(keys), preferred_element_type=jnp.float32
        )
        * scale
    )
    probs = masked_softmax(scores, key_ok, land_query)
    outs = jnp.einsum(
        "abhqk,abhkd->abhqd", probs, tiles(values), preferred_element_type=jnp.float32
    )
    outs = outs * (1.0 - land_query)[..., None]
    outs = outs.astype(jnp.bfloat16).reshape(rows // 8, cols // 8, nh, 8, 8, hd)
    return outs.transpose(0, 3, 1, 4, 2, 5).reshape(rows, cols, width)


def row_attend(query, keys, values, flags):
    rows, length, width = query.shape
    nh = HEADS
    hd = width // nh
    scale = hd ** (-0.5)
    key_ok = (flags > 0)[:, None, :]
    land_query = (flags <= 0).astype(jnp.float32)

    def head(index):
        qh = lax.dynamic_slice_in_dim(query, index * hd, hd, 2)
        kh = lax.dynamic_slice_in_dim(keys, index * hd, hd, 2)
        vh = lax.dynamic_slice_in_dim(values, index * hd, hd, 2)
        scores = jnp.einsum("rqd,rkd->rqk", qh, kh, preferred_element_type=jnp.float32) * scale
        probs = masked_softmax(scores, key_ok, land_query)
        return jnp.einsum("rqk,rkd->rqd", probs, vh, preferred_element_type=jnp.float32)

    outs = lax.map(head, jnp.arange(nh, dtype=jnp.int32))
    outs = outs.transpose(1, 2, 0, 3).reshape(rows, length, width)
    return (outs * (1.0 - land_query)[..., None]).astype(jnp.bfloat16)


def attend_columns(columns, marks, w_query1, w_key1, w_value1):
    return window_attend(
        project(columns, w_query1), project(columns, w_key1), project(columns, w_value1), marks
    )


def on_device(
    fields, ocean, w_query1, w_key1, w_value1, w_out1, w_query2, w_key2, w_value2, w_out2
):
    rows, cols, width = fields.shape
    normed = norm_rows(fields)
    marks = ocean.astype(jnp.bfloat16)
    edge_feats, edge_marks = passed_along((normed[:, cols - 4 :], marks[:, cols - 4 :]), "lon", 1)
    columns = jnp.concatenate([edge_feats, normed[:, : cols - 4]], 1)
    column_marks = jnp.concatenate([edge_marks, marks[:, : cols - 4]], 1)
    extended = attend_columns(columns, column_marks, w_query1, w_key1, w_value1)
    returned = passed_along(extended[:, :4], "lon", -1)
    o1 = jnp.concatenate([extended[:, 4:], returned], 1)
    y1 = (
        fields.astype(jnp.float32) + jnp.dot(o1, w_out1, preferred_element_type=jnp.float32)
    ).astype(jnp.bfloat16)
    h2 = norm_rows(y1)
    q2 = project(h2, w_query2)
    k2 = project(h2, w_key2)
    v2 = project(h2, w_value2)
    row_q, row_k, row_v, row_marks = (
        lax.all_to_all(q2, "lon", split_axis=0, concat_axis=1, tiled=True),
        lax.all_to_all(k2, "lon", split_axis=0, concat_axis=1, tiled=True),
        lax.all_to_all(v2, "lon", split_axis=0, concat_axis=1, tiled=True),
        lax.all_to_all(marks, "lon", split_axis=0, concat_axis=1, tiled=True),
    )
    row_out = row_attend(row_q, row_k, row_v, row_marks)
    o2 = lax.all_to_all(row_out, "lon", split_axis=1, concat_axis=0, tiled=True)
    return (
        y1.astype(jnp.float32) + jnp.dot(o2, w_out2, preferred_element_type=jnp.float32)
    ).astype(jnp.bfloat16)


def normed(af):
    mean = jnp.mean(af, -1, keepdims=True)
    diff = af - mean
    var = jnp.mean(diff * diff, -1, keepdims=True)
    return (diff * lax.rsqrt(var + EPS)).astype(jnp.bfloat16)


def mm(a, b):
    return jnp.dot(a, b, preferred_element_type=jnp.float32)


def pair_attend(q, k, v, bias, ocean_q, lane_a, ones):
    zero = jnp.zeros_like(k)
    kk = jnp.concatenate([jnp.where(lane_a, k, zero), jnp.where(lane_a, zero, k)], 0)
    s = lax.dot_general(q, kk, (((1,), (1,)), ((), ())), preferred_element_type=jnp.float32)
    fac = 1.4426950408889634 * 0.125
    probs = []
    for i in range(2):
        si = s[:, 128 * i : 128 * i + 128] + bias
        top = jnp.max(si, -1, keepdims=True)
        probs.append(jnp.exp2((si - top) * fac).astype(jnp.bfloat16))
    vv = jnp.concatenate([jnp.where(lane_a, v, zero), jnp.where(lane_a, zero, v)], 0)
    out = mm(jnp.concatenate(probs, 1), jnp.concatenate([vv, ones], 1))
    return (out[:, :128] * (ocean_q / (out[:, 128:] + (1.0 - ocean_q)))).astype(jnp.bfloat16)


D_ = 768
FLIPS = (4, 5, 6, 7, 2, 3, 1)

TURNS = (
    (0, 6, 2, 4), (1, 7, 5, 3), (0, 2, 6, 4), (1, 7, 5, 3),
    (0, 2, 4, 6), (1, 7, 3, 5), (0, 2, 4, 6), (1, 3, 7, 5),
)


def plan():
    bases, needs = [], []
    for rank, turns in enumerate(TURNS):
        seen, missing = set(), []
        for base in turns:
            fresh = [(base + k) % 8 for k in range(3) if (base + k) % 8 not in seen]
            seen.update(fresh)
            missing.append([(block + 4 * (rank // 4)) % 8 for block in fresh])
        bases.append([(base + 4 * (rank // 4)) % 8 for base in turns])
        needs.append(missing)
    return bases, needs


def flipped(index, flip):
    bits = [(index // 4) % 2, (index // 2) % 2, index % 2]
    total = 0
    for weight, bit in zip((4, 2, 1), bits):
        total = total + weight * ((1 - bit) if flip & weight else bit)
    return total


def band_kernel(
    x_ref, oc_ref, wq1, wk1, wv1, wo1, wq2, wk2, wv2, wo2, out_ref,
    x_buf, oc_out, oc_buf, win_buf, row_buf, w_buf, stage,
    y_ref, q_ref, k_ref, v_ref, q1_ref, k1_ref, v1_ref, o_ref,
    x_send, x_recv, oc_send, oc_recv, w_sem, z_send, z_recv,
):
    me = lax.axis_index("lon")
    mesh_id = pl.DeviceIdType.MESH
    peers = [flipped(me, flip) for flip in FLIPS]
    half, second = me // 4, (me // 2) % 2
    outer = (half + second + 1) % 2

    def pick(there, other):
        return outer * flipped(me, there) + (1 - outer) * flipped(me, other)

    far = [pick(4, 6), pick(5, 7), pick(6, 4), pick(7, 5)]
    x_order = [pick(3, 2), pick(2, 3), peers[6]] + far

    def ends(there, other):
        return (1 - second) * flipped(me, there) + second * flipped(me, other)

    soon = [ends(4, 6), ends(5, 7)]
    later = [ends(6, 4), ends(7, 5)]

    def send_x(to, landing):
        return pltpu.make_async_remote_copy(
            x_ref.at[to], x_buf.at[landing], x_send, x_recv.at[landing],
            device_id={"lon": to}, device_id_type=mesh_id,
        )

    def send_oc(to, landing):
        return pltpu.make_async_remote_copy(
            oc_out.at[to], oc_buf.at[landing], oc_send, oc_recv,
            device_id={"lon": to}, device_id_type=mesh_id,
        )

    def send_z(to, landing, c, count):
        return pltpu.make_async_remote_copy(
            stage.at[to, pl.ds(c, count)], out_ref.at[landing, pl.ds(c, count)],
            z_send, z_recv,
            device_id={"lon": to}, device_id_type=mesh_id,
        )

    def own_z(c):
        return pltpu.make_async_copy(stage.at[me, c], out_ref.at[me, c], z_recv)

    def taken(ref, sem):
        pltpu.make_async_copy(ref, ref, sem).wait()

    own_x = pltpu.make_async_copy(x_ref.at[me], x_buf.at[me], x_recv.at[me])
    own_oc = pltpu.make_async_copy(oc_out.at[me], oc_buf.at[me], oc_recv)
    weights = [
        pltpu.make_async_copy(w, w_buf.at[i], w_sem)
        for i, w in enumerate((wq1, wk1, wv1, wo1, wq2, wk2, wv2, wo2))
    ]

    barrier = pltpu.get_barrier_semaphore()
    for to in peers:
        pl.semaphore_signal(barrier, inc=1, device_id={"lon": to}, device_id_type=mesh_id)
    own_x.start()
    oc_out[...] = oc_ref[...].astype(jnp.float32).T.reshape(8, 8, 16)
    own_oc.start()
    pl.semaphore_wait(barrier, 7)
    for to in peers:
        send_oc(to, me).start()
    for to in x_order:
        send_x(to, me).start()
    for copy in weights:
        copy.start()

    tok_q = lax.broadcasted_iota(jnp.int32, (128, 128), 0)
    tok_k = lax.broadcasted_iota(jnp.int32, (128, 128), 1)
    same = ((tok_q // 8) % 2) == ((tok_k // 8) % 2)
    eye = tok_q == tok_k
    lane_a = lax.broadcasted_iota(jnp.int32, (128, 128), 1) < 64
    one = lane_a.astype(jnp.float32)
    ones = jnp.concatenate([one, 1.0 - one], 0).astype(jnp.bfloat16)
    col = lax.broadcasted_iota(jnp.int32, (1, 16, 768), 1)

    taken(oc_buf, oc_recv)
    lane = lax.broadcasted_iota(jnp.int32, (8, 128), 1)
    sub = lax.broadcasted_iota(jnp.int32, (8, 128), 0)
    by_row = jnp.concatenate([oc_buf[g] for g in range(8)], 1)
    by_row = pltpu.roll(by_row, 124, 1)
    by_window = jnp.zeros((8, 128), jnp.float32)
    for d in range(8):
        turned = pltpu.roll(by_row, 16 * d, 1) if d else by_row
        turned = jnp.where(lane // 16 == sub, turned, 0.0)
        by_window = by_window + (pltpu.roll(turned, 8 - d, 0) if d else turned)
    win_buf[...] = by_window
    row_buf[...] = by_row
    taken(w_buf, w_sem)

    def column_of(row_vec):
        return jnp.sum(jnp.where(eye, row_vec, 0.0), 1, keepdims=True)

    def arrived(source):
        taken(x_buf.at[source], x_recv.at[source])

    bases, needs = plan()

    def by_rank(values):
        total = 0
        for rank, value in enumerate(values):
            total = total + jnp.where(me == rank, value, 0)
        return total

    base_of = [by_rank([bases[rank][turn] for rank in range(8)]) for turn in range(4)]
    need_of = [
        [by_rank([needs[rank][turn][k] for rank in range(8)]) for k in range(count)]
        for turn, count in enumerate((3, 2, 2, 1))
    ]

    @pl.loop(0, 4)
    def _(i):
        def at_turn(values):
            total = 0
            for turn, value in enumerate(values):
                total = total + jnp.where(i == turn, value, 0)
            return total

        first = at_turn(base_of)
        arrived(at_turn([need[0] for need in need_of]))

        @pl.when(i == 0)
        def _():
            arrived(need_of[0][2])

        @pl.when(i < 3)
        def _():
            arrived(at_turn([need[1] for need in need_of[:3]]))

        parts = []
        for g in range(3):
            block = x_buf[(first + g) % 8].astype(jnp.float32)
            parts.append(pltpu.roll(block, 12, 1))
        x = jnp.concatenate(
            [jnp.where(col < 12, parts[g], parts[g + 1]).reshape(128, D_) for g in range(2)], 0
        )
        h = normed(x)
        q1_ref[...] = mm(h, w_buf[0]).astype(jnp.bfloat16)
        k1_ref[...] = mm(h, w_buf[1]).astype(jnp.bfloat16)
        v1_ref[...] = mm(h, w_buf[2]).astype(jnp.bfloat16)
        for g in range(2):
            flags = win_buf[pl.ds((first + g) % 8, 1), :]
            bias = jnp.where(jnp.logical_and(same, flags > 0), 0.0, NEG)
            ocean_q = jnp.broadcast_to(column_of(flags), (128, 128))
            rows = slice(128 * g, 128 * g + 128)
            for p in range(6):
                lanes = slice(128 * p, 128 * p + 128)
                o_ref[rows, lanes] = pair_attend(
                    q1_ref[rows, lanes], k1_ref[rows, lanes], v1_ref[rows, lanes],
                    bias, ocean_q, lane_a, ones,
                )
        y = (x + mm(o_ref[...], w_buf[3])).astype(jnp.bfloat16)
        h2 = normed(y.astype(jnp.float32))
        for keep, value in (
            (y_ref, y),
            (q_ref, mm(h2, w_buf[4]).astype(jnp.bfloat16)),
            (k_ref, mm(h2, w_buf[5]).astype(jnp.bfloat16)),
            (v_ref, mm(h2, w_buf[6]).astype(jnp.bfloat16)),
        ):
            for g in range(2):
                keep[(first + g) % 8] = value[128 * g : 128 * g + 128].reshape(8, 16, D_)

    @pl.loop(0, 8)
    def _(r):
        flags = row_buf[pl.ds(r, 1), :]
        bias = jnp.where(flags > 0, 0.0, NEG)
        ocean_q = jnp.broadcast_to(column_of(flags), (128, 128))
        for p in range(6):
            lanes = slice(128 * p, 128 * p + 128)
            o_ref[:128, lanes] = pair_attend(
                q_ref[:, r, :, lanes].reshape(128, 128),
                k_ref[:, r, :, lanes].reshape(128, 128),
                v_ref[:, r, :, lanes].reshape(128, 128),
                bias, ocean_q, lane_a, ones,
            )
        z = mm(o_ref[:128, :], w_buf[7])
        zr = z.reshape(8, 16, D_) + y_ref[:, r].astype(jnp.float32)
        zr = pltpu.roll(zr, 4, 1)
        before = jnp.concatenate([zr[7:], zr[:7]], 0)
        stage[:, r] = jnp.where(col < 4, before, zr).astype(jnp.bfloat16)
        for to in soon + peers[4:]:
            send_z(to, me, r, 1).start()
        own_z(r).start()

        @pl.when(jnp.logical_and(outer == 0, r % 4 == 3))
        def _():
            for to in later:
                send_z(to, me, r - 3, 4).start()

    @pl.when(outer == 1)
    def _():
        for to in later:
            send_z(to, me, 0, 8).start()


    taken(oc_buf.at[:7], oc_send)
    taken(x_buf.at[:7], x_send)
    taken(stage.at[:7], z_send)
    taken(out_ref, z_recv)


def on_bands(
    fields, ocean, w_query1, w_key1, w_value1, w_out1, w_query2, w_key2, w_value2, w_out2
):
    block = pltpu.VMEM((8, 8, 16, D_), jnp.bfloat16)
    part = pltpu.VMEM((256, D_), jnp.bfloat16)
    flags = pltpu.VMEM((8, 128), jnp.float32)
    sems = [(), (8,), (), (), (), (), ()]
    out = pl.pallas_call(
        band_kernel,
        out_shape=pltpu.VMEM((8, 8, 16, D_), jnp.bfloat16),
        in_specs=[pl.BlockSpec(memory_space=pltpu.HBM), pl.BlockSpec(memory_space=pltpu.VMEM)]
        + [pl.BlockSpec(memory_space=pltpu.HBM)] * 8,
        out_specs=pl.BlockSpec(memory_space=pl.ANY),
        scratch_shapes=[
            block,
            pltpu.VMEM((8, 8, 16), jnp.float32),
            pltpu.VMEM((8, 8, 16), jnp.float32),
            flags,
            flags,
            pltpu.VMEM((8, D_, D_), jnp.bfloat16),
            block,
        ]
        + [block] * 4
        + [part] * 4
        + [pltpu.SemaphoreType.DMA(shape) for shape in sems],
        compiler_params=pltpu.CompilerParams(
            vmem_limit_bytes=56 << 20, collective_id=0, has_side_effects=True
        ),
    )(
        fields.reshape(8, 8, 16, D_),
        ocean.T,
        w_query1, w_key1, w_value1, w_out1, w_query2, w_key2, w_value2, w_out2,
    )
    return out.reshape(64, 16, D_)


def solution(mesh):
    in_specs = (
        P(("grp", "lat"), "lon", None),
        P(("grp", "lat"), "lon"),
        P(),
        P(),
        P(),
        P(),
        P(),
        P(),
        P(),
        P(),
    )
    out_specs = P(("grp", "lat"), "lon", None)
    ranks = mesh.shape["lon"]

    def whole(fields, *rest):
        rows = fields.shape[0] // (mesh.shape["grp"] * mesh.shape["lat"])
        cols = fields.shape[1] // ranks
        banded = rows == 8 * ranks and cols == 16 and ranks == 8
        return jax.shard_map(
            on_bands if banded else on_device,
            mesh=mesh,
            in_specs=in_specs,
            out_specs=out_specs,
            check_vma=False,
        )(fields, *rest)

    return whole
```
